32 devices in a mesh: row: 8 (over y, x, core), col: 4 (over z).
Axes of the slice: x: 2, y: 2, z: 4, core: 2. Of those that a mesh axis runs over, the one named last changes fastest.
Arguments:
- slab: float32 [16384, 1536], P('row', 'col'), may hold values from -6 to 6
- hh_vectors: float32 [32, 512, 256], P('row', 'col'), may hold values from -0.25 to 0.25
- tfactors: float32 [32, 256, 256], P('row'), may hold values from -0.375 to 0.375
- plan: int32 [6, 8], P(None, 'row'), may hold values from 0 to 3
- offsets: int32 [6, 8], P(None, 'row'), may hold values from 256 to 1792, as said below
Outputs:
- result: float32 [16384, 1536], P('row', 'col')
The draws below stay inside these ranges and needn't reach their ends.
Inputs may be any that keep to these rules, and one draw needn't show every extreme that they name: offsets lie between 256 and 1792; in the last grid row they are at most 1536, so a window reaches at most 256 rows into the next grid row and the windows of one tick never meet. Where (t + r) % 4 == 0 and r is not the last grid row the offset is exactly 1792.
All inputs are finite; a program needn't handle non-finite values.
Results may differ from the reference program's by a relative error of at most 0.0003.
Values sent between devices are 32-bit elements; how exact they have to be, the bound alone decides.
No kernel may reach another device: no remote copies, remote signals or barrier semaphores. Data moves between devices by JAX's collectives and lax.ppermute only.
A program may use at most 64 MiB of HBM per device.

```python
import jax
import jax.numpy as jnp
from jax import lax

B = 256
R_DEV = 2048
GROUPS = 4
TICKS = 6
ROWS = 16384
COLS = 1536
N_ROW = 8


def draw_offsets(key, part):
    key_flag, key_cross, key_inner = jax.random.split(key, 3)
    ticks = jnp.arange(TICKS)[:, None]
    sections = jnp.arange(N_ROW)[None, :]
    flagged = jax.random.randint(key_flag, (TICKS, N_ROW), 0, 2)
    forced = (ticks + sections) % 4 == 0
    crossing = R_DEV - B - jax.random.randint(key_cross, (TICKS, N_ROW), 0, B)
    crossing = jnp.where(forced, R_DEV - B, crossing)
    interior = B + jax.random.randint(key_inner, (TICKS, N_ROW), 0, R_DEV - 3 * B + 1)
    chosen = ((flagged == 1) | forced) & (sections < N_ROW - 1)
    return jnp.where(chosen, crossing, interior).astype(jnp.int32)


def touch_ends(entries, key, low, high):
    extent = entries.shape
    spot = [jax.random.randint(jax.random.fold_in(key, axis), (), 0, extent[axis]) for axis in range(len(extent))]
    entries = entries.at[tuple(spot)].set(low)
    longest = extent.index(max(extent))
    spot[longest] = (spot[longest] + 1) % extent[longest]
    return entries.at[tuple(spot)].set(high)


def level_of(stream_key, dims, pieces, low, high):
    level = 1.0
    for dim, parts in pieces:
        steps = jax.random.uniform(jax.random.fold_in(jax.random.fold_in(stream_key, 6), dim), (parts,), jnp.float32, low / len(pieces), high / len(pieces))
        level = level * jnp.repeat(jnp.exp(steps), dims[dim] // parts).reshape((-1,) + (1,) * (len(dims) - 1 - dim))
    return level


def normal_values(rng, shape, deviation, bound, cuts=(), dtype=jnp.bfloat16):
    result = jax.random.normal(rng, shape, jnp.float32) * deviation
    if len(cuts) > 0:
        result = level_of(rng, shape, cuts, -0.22, 0.18) * result
    return jnp.clip(result, min=-bound, max=bound).astype(dtype)


def setup_inputs(seed: int = 0) -> dict:
    streams_of = jax.random.split(jax.random.key(seed), 6)
    return {
        "slab": normal_values(streams_of[0], (ROWS, COLS), 1.0, 6.0, ((0, 8), (1, 4)), jnp.float32),
        "hh_vectors": normal_values(streams_of[1], (N_ROW * GROUPS, 2 * B, B), (2 * B) ** -0.5, 0.25, ((0, 8), (1, 4)), jnp.float32),
        "tfactors": normal_values(streams_of[2], (N_ROW * GROUPS, B, B), B ** -0.5, 0.375, ((0, 8),), jnp.float32),
        "plan": touch_ends(jax.random.randint(streams_of[3], (TICKS, N_ROW), 0, GROUPS), jax.random.fold_in(streams_of[3], 1), 0, GROUPS - 1).astype(jnp.int32),
        "offsets": draw_offsets(jax.random.fold_in(streams_of[5], 71), 0),
    }


def reference(slab, hh_vectors, tfactors, plan, offsets):
    hp = lax.Precision.HIGHEST
    cols = slab.shape[1]

    def apply_section(r, state):
        x, t = state
        g = (r * GROUPS + plan[t, r]).astype(jnp.int32)
        vec = lax.dynamic_index_in_dim(hh_vectors, g, 0, keepdims=False)
        tf = lax.dynamic_index_in_dim(tfactors, g, 0, keepdims=False)
        start = (r * R_DEV + offsets[t, r]).astype(jnp.int32)
        window = lax.dynamic_slice(x, (start, jnp.int32(0)), (2 * B, cols))
        inner = jnp.dot(vec.T, window, precision=hp, preferred_element_type=jnp.float32)
        inner = jnp.dot(tf, inner, precision=hp, preferred_element_type=jnp.float32)
        window = window - jnp.dot(vec, inner, precision=hp, preferred_element_type=jnp.float32)
        x = lax.dynamic_update_slice(x, window, (start, jnp.int32(0)))
        return (x, t)

    x = slab
    for tick in range(TICKS):
        x, _ = lax.fori_loop(0, N_ROW, apply_section, (x, jnp.int32(tick)))
    return x
```

```python
import functools

import jax
import jax.numpy as jnp
from jax import lax
from jax.experimental import pallas as pl
from jax.experimental.pallas import tpu as pltpu
from jax.sharding import PartitionSpec as P


LANES = 128
NT = (((1,), (1,)), ((), ()))
NN = (((1,), (0,)), ((), ()))


def split(value):
    high = value.astype(jnp.bfloat16)
    low = (value - high.astype(jnp.float32)).astype(jnp.bfloat16)
    return high, low


def product(a, b, dims):
    (ah, al), (bh, bl) = a, b
    dot = functools.partial(lax.dot_general, dimension_numbers=dims, preferred_element_type=jnp.float32)
    return dot(ah, bh) + (dot(ah, bl) + dot(al, bh))


def ticks_kernel(n_col, n_plus, *refs):
    plan, offsets, slab, held, tfactors, own = refs[:6]
    received = refs[6 : 6 + 2 * n_plus]
    out, boundary, x, tf, vf, vh, vl, uh, ul, sems, vsem = refs[6 + 2 * n_plus :]
    ticks = plan.shape[0]
    tiles, rows, _ = x.shape
    groups, rank, band = vf.shape
    depth = own.shape[1]
    me = lax.axis_index("col")

    def rows_of(j):
        return vf.at[:, pl.ds(pl.multiple_of(j * depth, depth), depth), :]

    loads = []
    for c in range(tiles):
        cols = pl.ds(c * LANES, LANES)
        loads.append(pltpu.make_async_copy(slab.at[pl.ds(band, rows - band), cols], x.at[c, pl.ds(0, rows - band)], sems.at[c]))
        loads.append(pltpu.make_async_copy(held.at[:, cols], x.at[c, pl.ds(rows - band, band)], sems.at[tiles + c]))
    loads.append(pltpu.make_async_copy(tfactors, tf, sems.at[2 * tiles]))
    pltpu.make_async_copy(own, rows_of(me), vsem).start()
    for s in range(n_plus):

        @pl.when(me - 1 - s >= 0)
        def _():
            pltpu.make_async_copy(received[s], rows_of(me - 1 - s), vsem).start()

        @pl.when(me + 1 + s < n_col)
        def _():
            pltpu.make_async_copy(received[n_plus + s], rows_of(me + 1 + s), vsem).start()

    for load in loads:
        load.start()
    pltpu.make_async_copy(vf, vf, vsem).wait()
    for load in loads:
        load.wait()

    @pl.loop(0, groups)
    def _(g):
        v = split(vf[g])
        vh[g], vl[g] = v
        uh[g], ul[g] = split(product(split(tf[g]), v, NT))

    @pl.loop(0, ticks)
    def _(t):
        g = plan[t, 0]
        window = pl.ds(offsets[t, 0] - band, rank)
        w = jnp.concatenate([x[c, window] for c in range(tiles)], axis=1)
        y = product((uh[g], ul[g]), split(w), NN)
        update = product((vh[g], vl[g]), split(y), NN)
        w = w - update
        for c in range(tiles):
            x[c, window] = w[:, c * LANES : (c + 1) * LANES]

    stores = []
    for c in range(tiles):
        cols = pl.ds(c * LANES, LANES)
        stores.append(pltpu.make_async_copy(x.at[c, pl.ds(0, rows - band)], out.at[pl.ds(band, rows - band), cols], sems.at[c]))
        stores.append(pltpu.make_async_copy(x.at[c, pl.ds(rows - band, band)], boundary.at[:, cols], sems.at[tiles + c]))
    for store in stores:
        store.start()
    for store in stores:
        store.wait()


def all_ticks(slab, held, tfactors, own, received, plan, offsets, n_col):
    rows, cols = slab.shape
    groups, depth, band = own.shape
    rank = n_col * depth
    tiles = cols // LANES
    anywhere = pl.BlockSpec(memory_space=pl.ANY)
    scalars = pl.BlockSpec(memory_space=pltpu.SMEM)
    return pl.pallas_call(
        functools.partial(ticks_kernel, n_col, len(received) // 2),
        out_shape=(
            jax.ShapeDtypeStruct((rows, cols), jnp.float32),
            jax.ShapeDtypeStruct((band, cols), jnp.float32),
        ),
        in_specs=[scalars, scalars] + [anywhere] * (4 + len(received)),
        out_specs=(anywhere, anywhere),
        scratch_shapes=[
            pltpu.VMEM((tiles, rows, LANES), jnp.float32),
            pltpu.VMEM((groups, band, band), jnp.float32),
            pltpu.VMEM((groups, rank, band), jnp.float32),
            pltpu.VMEM((groups, rank, band), jnp.bfloat16),
            pltpu.VMEM((groups, rank, band), jnp.bfloat16),
            pltpu.VMEM((groups, band, rank), jnp.bfloat16),
            pltpu.VMEM((groups, band, rank), jnp.bfloat16),
            pltpu.SemaphoreType.DMA((2 * tiles + 1,)),
            pltpu.SemaphoreType.DMA(()),
        ],
        compiler_params=pltpu.CompilerParams(vmem_limit_bytes=40 << 20),
    )(plan, offsets, slab, held, tfactors, own, *received)


def shards(slab, hh_vectors, tfactors, plan, offsets):
    band = tfactors.shape[1]
    n_row, n_col = lax.axis_size("row"), lax.axis_size("col")
    upward = [(i, (i - 1) % n_row) for i in range(n_row)]
    downward = [(i, (i + 1) % n_row) for i in range(n_row)]
    held = lax.ppermute(slab[:band], "row", upward)
    plus, minus = [hh_vectors], [hh_vectors]
    for s in range(n_col - 1):
        plus.append(lax.ppermute(plus[-1], "col", [(i, i + 1) for i in range(s, n_col - 1)]))
        minus.append(lax.ppermute(minus[-1], "col", [(i, i - 1) for i in range(1, n_col - s)]))
    out, boundary = all_ticks(slab, held, tfactors, hh_vectors, plus[1:] + minus[1:], plan, offsets, n_col)
    head = lax.ppermute(boundary, "row", downward)
    return lax.dynamic_update_slice(out, head, (0, 0))


def solution(mesh):
    placed = (
        P("row", "col"),
        P("row", "col", None),
        P("row", None, None),
        P(None, "row"),
        P(None, "row"),
    )
    return jax.shard_map(
        shards, mesh=mesh, in_specs=placed, out_specs=P("row", "col"), check_vma=False
    )
```

```python
import functools

import jax
import jax.numpy as jnp
from jax import lax
from jax.experimental import pallas as pl
from jax.experimental.pallas import tpu as pltpu
from jax.sharding import PartitionSpec as P


LANES = 128
NT = (((1,), (1,)), ((), ()))
NN = (((1,), (0,)), ((), ()))
ANYWHERE = pl.BlockSpec(memory_space=pl.ANY)
OFF_CHIP = pl.BlockSpec(memory_space=pltpu.HBM)
ON_CHIP = pl.BlockSpec(memory_space=pltpu.VMEM)
SCALARS = pl.BlockSpec(memory_space=pltpu.SMEM)
PARAMS = pltpu.CompilerParams(vmem_limit_bytes=16 << 20)


def on_chip(*arrays):
    return [pltpu.with_memory_space_constraint(a, pltpu.VMEM) for a in arrays]


def off_chip(array):
    return pltpu.with_memory_space_constraint(array, pltpu.HBM)


def split(value):
    high = value.astype(jnp.bfloat16)
    low = (value - high.astype(jnp.float32)).astype(jnp.bfloat16)
    return high, low


def product(a, b, dims):
    (ah, al), (bh, bl) = a, b
    dot = functools.partial(lax.dot_general, dimension_numbers=dims, preferred_element_type=jnp.float32)
    return dot(ah, bh) + (dot(ah, bl) + dot(al, bh))


def slots(plan, groups):
    ticks = plan.shape[1]
    first = []
    for g in range(groups):
        at = jnp.int32(ticks)
        for t in reversed(range(ticks)):
            at = jnp.where(plan[0, t] == g, t, at)
        first.append(at)
    slot_of = []
    for g in range(groups):
        slot = jnp.int32(0)
        for h in range(groups):
            if h != g:
                ahead = first[h] <= first[g] if h < g else first[h] < first[g]
                slot = slot + ahead.astype(jnp.int32)
        slot_of.append(slot)
    group_of, starts = [], []
    for s in range(groups):
        group, start = jnp.int32(0), jnp.int32(0)
        for g in range(groups):
            here = slot_of[g] == s
            group = jnp.where(here, g, group)
            start = jnp.where(here, first[g], start)
        group_of.append(group)
        starts.append(start)
    return slot_of, group_of, starts


def pack_kernel(plan, own, *refs):
    chunks, sems = refs[:-1], refs[-1]
    _, group_of, _ = slots(plan, own.shape[0])
    copies, s = [], 0
    for chunk in chunks:
        for k in range(chunk.shape[0]):
            copies.append(pltpu.make_async_copy(own.at[group_of[s]], chunk.at[k], sems.at[s]))
            s += 1
    for copy in copies:
        copy.start()
    for copy in copies:
        copy.wait()


def load_kernel(slab, held, tfactors, x, tf, sems):
    tiles, rows, _ = x.shape
    band = held.shape[0]
    copies = [pltpu.make_async_copy(tfactors, tf, sems.at[tiles])]
    for c in range(tiles):
        copies.append(pltpu.make_async_copy(slab.at[pl.ds(band, rows - band), pl.ds(c * LANES, LANES)], x.at[c, pl.ds(0, rows - band)], sems.at[c]))
    for copy in copies:
        copy.start()
    for c in range(tiles):
        x[c, pl.ds(rows - band, band)] = held[:, c * LANES : (c + 1) * LANES]
    for copy in copies:
        copy.wait()


def ticks_kernel(base, last, n_col, *refs):
    plan, offsets, tf, own = refs[:4]
    refs = refs[4:]
    plus, minus, refs = refs[: n_col - 1], refs[n_col - 1 : 2 * n_col - 2], refs[2 * n_col - 2 :]
    earlier, refs = (refs[:4], refs[4:]) if base else (None, refs)
    x, vh, vl, uh, ul = refs[1:6]
    boundary = refs[6] if last else None
    ticks = plan.shape[1]
    tiles, rows, _ = x.shape
    size, depth, band = own.shape
    me = lax.axis_index("col")
    slot_of, group_of, starts = slots(plan, tf.shape[0])

    sources = [me] + [jnp.where(me > s, me - 1 - s, me + n_col - 1 - s) for s in range(n_col - 1)]
    if base:
        for old, new in zip(earlier, (vh, vl, uh, ul)):
            new[:base] = old[...]
    for k in range(size):
        s = base + k
        v = [own[k]] + [jnp.where(me > i, plus[i][k], minus[n_col - 2 - i][k]) for i in range(n_col - 1)]
        v = split(jnp.concatenate(v, axis=0))
        vh[s], vl[s] = v
        uh[s], ul[s] = split(product(split(tf[group_of[s]]), v, NT))

    def tick(t, carry):
        slot = jnp.int32(0)
        for g in range(len(slot_of)):
            slot = jnp.where(plan[0, t] == g, slot_of[g], slot)
        top = offsets[0, t] - band
        at = [pl.ds(top + source * depth, depth) for source in sources]
        w = jnp.concatenate([jnp.concatenate([x[c, rows_] for c in range(tiles)], axis=1) for rows_ in at], axis=0)
        y = product((uh[slot], ul[slot]), split(w), NN)
        w = w - product((vh[slot], vl[slot]), split(y), NN)
        for i, rows_ in enumerate(at):
            for c in range(tiles):
                x[c, rows_] = w[i * depth : (i + 1) * depth, c * LANES : (c + 1) * LANES]
        return carry

    begin = starts[base] if base else 0
    end = ticks if last else starts[base + size]
    lax.fori_loop(begin, end, tick, 0)
    if last:
        for c in range(tiles):
            boundary[:, c * LANES : (c + 1) * LANES] = x[c, pl.ds(rows - band, band)]


def store_kernel(band, x, out, sems):
    tiles, rows, _ = x.shape
    copies = []
    for c in range(tiles):
        copies.append(pltpu.make_async_copy(x.at[c, pl.ds(0, rows - band)], out.at[pl.ds(band, rows - band), pl.ds(c * LANES, LANES)], sems.at[c]))
    for copy in copies:
        copy.start()
    for copy in copies:
        copy.wait()


def shards(sizes, slab, hh_vectors, tfactors, plan, offsets):
    rows, cols = slab.shape
    groups, depth, band = hh_vectors.shape
    tiles = cols // LANES
    n_row, n_col = lax.axis_size("row"), lax.axis_size("col")
    rank = n_col * depth
    plan, offsets = plan.T, offsets.T
    f32, bf16 = jnp.float32, jnp.bfloat16

    chunks = pl.pallas_call(
        pack_kernel,
        out_shape=tuple(pltpu.VMEM((size, depth, band), f32) for size in sizes),
        in_specs=[SCALARS, OFF_CHIP],
        out_specs=tuple(ON_CHIP for _ in sizes),
        scratch_shapes=[pltpu.SemaphoreType.DMA((groups,))],
        compiler_params=PARAMS,
        name="pack",
    )(plan, off_chip(hh_vectors))

    plus, minus = [[chunk] for chunk in chunks], [[chunk] for chunk in chunks]
    for s in range(n_col - 1):
        for p, m in zip(plus, minus):
            p.append(lax.ppermute(p[-1], "col", [(i, i + 1) for i in range(s, n_col - 1)]))
            m.append(lax.ppermute(m[-1], "col", [(i, i - 1) for i in range(1, n_col - s)]))
    held = lax.ppermute(slab[:band], "row", [(i, (i - 1) % n_row) for i in range(n_row)])

    x, tf = pl.pallas_call(
        load_kernel,
        out_shape=(pltpu.VMEM((tiles, rows, LANES), f32), pltpu.VMEM(tfactors.shape, f32)),
        in_specs=[OFF_CHIP, ON_CHIP, OFF_CHIP],
        out_specs=(ON_CHIP, ON_CHIP),
        scratch_shapes=[pltpu.SemaphoreType.DMA((tiles + 1,))],
        compiler_params=PARAMS,
        name="load",
    )(off_chip(slab), *on_chip(held), off_chip(tfactors))

    factors, boundary, base = [], None, 0
    for size, p, m in zip(sizes, plus, minus):
        last = base + size == groups
        held_slots = base + size
        out_shape = [pltpu.VMEM(x.shape, f32)]
        out_shape += [pltpu.VMEM((held_slots, rank, band), bf16)] * 2
        out_shape += [pltpu.VMEM((held_slots, band, rank), bf16)] * 2
        if last:
            out_shape.append(pltpu.VMEM((band, cols), f32))
        operands = on_chip(tf, p[0], *p[1:], *m[1:], *factors, x)
        results = pl.pallas_call(
            functools.partial(ticks_kernel, base, last, n_col),
            out_shape=tuple(out_shape),
            in_specs=[SCALARS, SCALARS] + [ON_CHIP] * len(operands),
            out_specs=tuple(ON_CHIP for _ in out_shape),
            input_output_aliases={len(operands) + 1: 0},
            compiler_params=PARAMS,
            name="ticks",
        )(plan, offsets, *operands)
        x, factors = results[0], list(results[1:5])
        base += size
    boundary = results[5]
    head = lax.ppermute(boundary, "row", [(i, (i + 1) % n_row) for i in range(n_row)])
    out = pl.pallas_call(
        functools.partial(store_kernel, band),
        out_shape=jax.ShapeDtypeStruct((rows, cols), f32),
        in_specs=[ON_CHIP],
        out_specs=ANYWHERE,
        scratch_shapes=[pltpu.SemaphoreType.DMA((tiles,))],
        compiler_params=PARAMS,
        name="store",
    )(*on_chip(x))
    return lax.dynamic_update_slice(out, head, (0, 0))


def solution(mesh):
    placed = (
        P("row", "col"),
        P("row", "col", None),
        P("row", None, None),
        P(None, "row"),
        P(None, "row"),
    )
    return jax.shard_map(
        functools.partial(shards, (2, 2)),
        mesh=mesh,
        in_specs=placed,
        out_specs=P("row", "col"),
        check_vma=False,
    )
```
